32 devices in a mesh: groups: 2 (over x), dp: 16 (over z, y, core).
Axes of the slice: x: 2, y: 2, z: 4, core: 2. Of those that a mesh axis runs over, the one named last changes fastest.
Arguments:
- tokens: bfloat16 [12288, 8192], P(('groups', 'dp')), parts along dimension 0, may hold values from -6 to 6
- base_weight: bfloat16 [8192, 768], P('dp'), may hold values from -0.0625 to 0.0625
- down_stack: bfloat16 [8192, 512], P('dp'), may hold values from -0.0625 to 0.0625
- up_stack: bfloat16 [512, 768], replicated, may hold values from -0.75 to 0.75
- adapter_scale: float32 [8], replicated, may hold values from 0.5 to 2
- lengths: int32 [64], P(('groups', 'dp')), parts along dimension 0, may hold values from 1 to 256, as said below
- adapter_ids: int32 [64], P(('groups', 'dp')), parts along dimension 0, may hold values from 0 to 7
Outputs:
- projected: bfloat16 [12288, 768], P(('groups', 'dp')), parts along dimension 0
The draws below stay inside these ranges and needn't reach their ends.
There are 2 independent parts, one for each index of `groups`. The reference program is written for one: setup_inputs(seed, part) draws one part's arguments, and reference() takes and returns one part's arrays. A program takes and returns all parts, laid end to end along the dimension named above; an argument that names none is the same for every part. Nothing has to cross between parts.
Inputs may be any that keep to these rules, and one draw needn't show every extreme that they name: `lengths`: each index of dp holds two requests whose block counts ceil(length / 128) add up to exactly 3.
All inputs are finite; a program needn't handle non-finite values.
Results may differ from the reference program's by a relative error of at most 0.0042.
Values may be sent and summed in bfloat16 or wider, within the bound.
A program may use at most 128 MiB of HBM per device.

```python
import math
from functools import partial
import jax
import jax.numpy as jnp

D = 8192
RANK = 64
ADAPTERS = 8
BLOCK = 128
BLOCKS_DEV = 3
COLS = 768
TOK_DEV = 384
TOKENS = 6144
REQUESTS = 32
N_DP = 16


def draw_lengths(key, part):
    key_first, key_rest = jax.random.split(jax.random.fold_in(key, 11))
    pair_count = REQUESTS // 2
    first = jax.random.randint(key_first, (pair_count,), 1, BLOCKS_DEV)
    first = first.at[0].set(BLOCKS_DEV - 1)
    counts = jnp.stack([first, BLOCKS_DEV - first], axis=1)
    remainders = jax.random.randint(key_rest, (pair_count, 2), 1, BLOCK + 1)
    remainders = remainders.at[0, 0].set(BLOCK).at[0, 1].set(1)
    return ((counts - 1) * BLOCK + remainders).reshape(REQUESTS).astype(jnp.int32)


def touch_ends(array, own_key, low, top_value):
    longest = array.shape.index(max(array.shape))
    spots = []
    for shift in (0, 1):
        where = [jax.random.randint(jax.random.fold_in(own_key, axis), (), 0, length) for axis, length in enumerate(array.shape)]
        where[longest] = (where[longest] + shift) % array.shape[longest]
        spots.append(tuple(where))
    return array.at[spots[0]].set(low).at[spots[1]].set(top_value)


def levels(own_key, dims, cuts, low, top_value):
    loudness = 1.0
    for axis_at, blocks in cuts:
        steps = jax.random.uniform(jax.random.fold_in(jax.random.fold_in(own_key, 6), axis_at), (blocks,), jnp.float32, low / len(cuts), top_value / len(cuts))
        loudness = loudness * jnp.repeat(jnp.exp(steps), dims[axis_at] // blocks).reshape((-1,) + (1,) * (len(dims) - 1 - axis_at))
    return loudness


def noise(rng, extent, deviation, limit, cuts=(), kind=jnp.bfloat16):
    array = deviation * jax.random.normal(rng, extent, jnp.float32)
    if cuts:
        array = array * levels(rng, extent, cuts, -0.22, 0.18)
    return jnp.clip(array, -limit, limit).astype(kind)


def setup_inputs(seed: int = 0, part: int = 0) -> dict:
    keys = jax.random.split(jax.random.key(seed), 8)
    own_keys = jax.random.split(jax.random.fold_in(keys[7], part), 8)
    return {
        "tokens": noise(own_keys[0], (TOKENS, D), 1.0, 6.0, ((0, 16),)),
        "base_weight": noise(keys[1], (D, COLS), D ** -0.5, 0.0625, ((0, 16),)),
        "down_stack": noise(keys[2], (D, ADAPTERS * RANK), D ** -0.5, 0.0625, ((0, 16),)),
        "up_stack": noise(keys[3], (ADAPTERS * RANK, COLS), RANK ** -0.5, 0.75),
        "adapter_scale": jnp.clip(jnp.exp(jax.random.uniform(keys[4], (ADAPTERS,), jnp.float32, math.log(0.5), math.log(2.0))), 0.5, 2.0),
        "lengths": draw_lengths(jax.random.fold_in(jax.random.fold_in(keys[7], part), 71), part),
        "adapter_ids": touch_ends(jax.random.randint(own_keys[6], (REQUESTS,), 0, ADAPTERS), jax.random.fold_in(own_keys[6], 1), 0, ADAPTERS - 1).astype(jnp.int32),
    }


def layout(lengths, adapter_ids, row_count):
    counts = (lengths + BLOCK - 1) // BLOCK
    position = jnp.arange(row_count, dtype=jnp.int32)
    boundary = counts[0] * BLOCK
    second = position >= boundary
    offset = jnp.where(second, position - boundary, position)
    is_live = offset < jnp.where(second, lengths[1], lengths[0])
    token_adapter = jnp.where(second, adapter_ids[1], adapter_ids[0])
    return is_live, token_adapter.astype(jnp.int32)


def reference(tokens, base_weight, down_stack, up_stack, adapter_scale, lengths, adapter_ids):
    is_live, token_adapter = jax.vmap(partial(layout, row_count=TOK_DEV))(
        lengths.reshape(N_DP, 2), adapter_ids.reshape(N_DP, 2))
    is_live = is_live.reshape(-1)
    token_adapter = token_adapter.reshape(-1)
    base_out = jnp.dot(tokens, base_weight, preferred_element_type=jnp.float32)
    onehot = (token_adapter[:, None] == jnp.arange(ADAPTERS, dtype=jnp.int32)[None, :]).astype(jnp.float32)
    every_down_weight = jnp.dot(tokens, down_stack, preferred_element_type=jnp.float32).reshape(-1, ADAPTERS, RANK)
    low_rank = jnp.sum(onehot[:, :, None] * every_down_weight, axis=1).astype(jnp.bfloat16)
    widened = (onehot[:, :, None].astype(jnp.bfloat16) * low_rank[:, None, :]).reshape(-1, ADAPTERS * RANK)
    adapter_out = jnp.dot(widened, up_stack, preferred_element_type=jnp.float32)
    token_scale = jnp.sum(onehot * adapter_scale[None, :], axis=1)
    result = jnp.where(is_live[:, None], base_out + token_scale[:, None] * adapter_out, 0.0)
    return result.astype(jnp.bfloat16)
```

```python
import functools

import jax
import jax.numpy as jnp
from jax import lax
from jax.experimental import pallas as pl
from jax.experimental.pallas import tpu as pltpu
from jax.sharding import PartitionSpec as P

BLOCK = 128
PIECE = 32
MESH = pl.DeviceIdType.MESH


def plan(depth, pieces, special, first):
    gathered = pieces - special
    queues = {
        (z, d): []
        for z in range(depth)
        for d in "udyx"
        if not (d == "u" and z == depth - 1) and not (d == "d" and z == 0)
    }

    def targets(piece, via):
        if via == "x":
            return ""
        if piece in first:
            out = {"own": "udy", "y": "ud", "u": "u", "d": "d"}[via]
        else:
            out = {"own": "udy", "y": "", "u": "uy", "d": "dy"}[via]
        return out + "x" if piece < special and via != "own" else out

    own = [targets(k, "own") for k in range(gathered)]
    for z in range(depth):
        for k in range(gathered):
            for d in own[k]:
                if (z, d) in queues:
                    queues[z, d].append((z, 1, k))
    events = [[] for _ in range(depth)]
    while any(queues.values()):
        moved = [(z, d, q.pop(0)) for (z, d), q in queues.items() if q]
        for z, d, (owner, same, k) in sorted(moved, key=lambda m: "udyx".index(m[1])):
            at = z + (d == "u") - (d == "d")
            if d == "y":
                same = 1 - same
            out = "".join(o for o in targets(k, d) if (at, o) in queues)
            for o in out:
                queues[at, o].append((owner, same, k))
            events[at].append((d, owner, same, k, out))
    return events


def kernel(
    sizes, tok_hbm, base_hbm, down_hbm, up_hbm, scale_ref, len_ref, ids_ref, out_ref,
    held, tok, up, acc, load_sem, recv_sem, send_sem, own_sem, core_recv, core_send,
):
    depth, special, first, swap = sizes
    rows, base_cols = base_hbm.shape
    pieces = rows // PIECE
    gathered = pieces - special
    events = plan(depth, pieces, special, first)
    group, me = lax.axis_index("groups"), lax.axis_index("dp")
    core, y, z = me % 2, (me // 2) % 2, me // 4
    side = group % 2
    at = [z == k for k in range(depth)]

    def pick(values):
        if len(set(values)) == 1:
            return values[0]
        out = jnp.int32(values[0])
        for k in range(1, depth):
            if values[k] != values[0]:
                out = jnp.where(at[k], jnp.int32(values[k]), out)
        return out

    def when(flags, fn):
        if all(flags):
            fn()
        elif any(flags):
            pl.when(pick([int(f) for f in flags]) == 1)(fn)

    peers = {
        "u": (group, me + 4),
        "d": (group, me - 4),
        "y": (group, me + 2 - 4 * y),
        "x": (group + 1 - 2 * side, me),
        "p": (group, me + 1 - 2 * core),
    }
    has = {
        "u": [k < depth - 1 for k in range(depth)],
        "d": [k > 0 for k in range(depth)],
        "y": [True] * depth,
        "x": [swap] * depth,
        "p": [True] * depth,
    }
    kinds = "udyx"

    pair = z * 2 + y
    mine = pl.multiple_of(me * rows, rows)
    loads = [
        pltpu.make_async_copy(base_hbm, held.at[pl.ds(mine, rows), pl.ds(0, base_cols)], load_sem.at[0]),
        pltpu.make_async_copy(
            down_hbm, held.at[pl.ds(mine, rows), pl.ds(base_cols, down_hbm.shape[1])], load_sem.at[1]
        ),
        pltpu.make_async_copy(tok_hbm, tok, load_sem.at[2]),
        pltpu.make_async_copy(up_hbm, up, load_sem.at[3]),
    ]
    for load in loads:
        load.start()

    barrier = pltpu.get_barrier_semaphore()
    for d in "udyxp":
        def greet(d=d):
            pl.semaphore_signal(barrier, inc=1, device_id=peers[d], device_id_type=MESH)
        when(has[d], greet)
    pl.semaphore_wait(barrier, pick([sum(has[d][k] for d in "udyxp") for k in range(depth)]))

    def copy(d, start, count, send, recv):
        piece = held.at[pl.ds(start, count)]
        return pltpu.make_async_remote_copy(
            src_ref=piece, dst_ref=piece, send_sem=send, recv_sem=recv,
            device_id=peers[d], device_id_type=MESH,
        )

    loads[0].wait()
    loads[1].wait()
    for k in range(gathered):
        sub = k + side * special if k < special else special + k
        start = pl.multiple_of(mine + sub * PIECE, PIECE)
        for i, d in enumerate("udy"):
            def send(i=i, d=d, start=start, sub=sub):
                copy(d, start, PIECE, own_sem.at[i], recv_sem.at[pair, sub]).start()
            when(has[d], send)
    copy("p", mine, rows, core_send.at[pair], core_recv.at[pair]).start()

    cols = held.shape[1]
    step = cols // 5 if cols % 5 == 0 else cols

    def multiply(which, fresh):
        copy("p", 0, rows, core_send.at[which], core_recv.at[which]).wait_recv()
        span = pl.ds(pl.multiple_of(which * (2 * rows), 2 * rows), 2 * rows)
        left = tok[:, span]

        @pl.loop(0, cols // step)
        def _(n):
            part = pl.ds(pl.multiple_of(n * step, step), step)
            term = jnp.dot(left, held[span, part], preferred_element_type=jnp.float32)
            acc[:, part] = term if fresh else acc[:, part] + term

    seen = [{} for _ in range(depth)]
    done = [[] for _ in range(depth)]
    total = len(events[0])
    for e in range(total):
        row = [events[k][e] for k in range(depth)]
        owner = pick([r[1] for r in row])
        same = pick([r[2] for r in row])
        offset, slope = [], []
        for r in row:
            if r[0] == "x":
                offset.append(special + r[3])
                slope.append(-special)
            elif r[3] < special:
                offset.append(r[3])
                slope.append(special)
            else:
                offset.append(special + r[3])
                slope.append(0)
        sub = pick(offset) + pick(slope) * side
        which = owner * 2 + (1 - same) + (2 * same - 1) * y
        start = pl.multiple_of((which * 2 + core) * rows + sub * PIECE, PIECE)
        arrived = recv_sem.at[which, sub]
        copy("p", start, PIECE, core_send.at[which], arrived).wait_recv()
        for i, d in enumerate(kinds):
            def relay(i=i, d=d, start=start, which=which, arrived=arrived):
                copy(d, start, PIECE, send_sem.at[i, which], arrived).start()
            when([d in r[4] for r in row], relay)
        copy("p", start, PIECE, core_send.at[which], core_recv.at[which]).start()
        if e == 4:
            loads[2].wait()
            multiply(pair, True)
        for k in range(depth):
            key = row[k][1:3]
            seen[k][key] = seen[k].get(key, 0) + 1
            if seen[k][key] == pieces:
                done[k].append((e, key))
        n = min(len(d) for d in done)
        if n and max(d[n - 1][0] for d in done) == e:
            fresh_done = [m for m in range(n) if max(d[m][0] for d in done) == e]
            for m in fresh_done:
                owners = pick([d[m][1][0] for d in done])
                sames = pick([d[m][1][1] for d in done])
                multiply(owners * 2 + (1 - sames) + (2 * sames - 1) * y, False)

    loads[3].wait()
    tokens = acc.shape[0]
    adapters = scale_ref.shape[0]
    rank = (cols - base_cols) // adapters
    boundary = ((len_ref[0] + (BLOCK - 1)) // BLOCK) * BLOCK
    position = lax.broadcasted_iota(jnp.int32, (tokens, 1), 0)
    second = position >= boundary
    offsets = jnp.where(second, position - boundary, position)
    live = offsets < jnp.where(second, len_ref[1], len_ref[0])
    low = jnp.where(second, ids_ref[1], ids_ref[0]) * rank
    scale = jnp.where(second, scale_ref[ids_ref[1]], scale_ref[ids_ref[0]])
    lane = lax.broadcasted_iota(jnp.int32, (tokens, cols - base_cols), 1)
    chosen = (lane >= low) & (lane < low + rank)
    widened = jnp.where(chosen, acc[:, base_cols:], 0.0).astype(jnp.bfloat16)
    width = base_cols // 3
    for n in range(3):
        part = slice(n * width, (n + 1) * width)
        adapter_out = jnp.dot(widened, up[:, part], preferred_element_type=jnp.float32)
        out_ref[:, part] = jnp.where(live, acc[:, part] + scale * adapter_out, 0.0).astype(out_ref.dtype)

    for i in range(3):
        def sent(i=i):
            copy("udy"[i], 0, gathered * PIECE, own_sem.at[i], recv_sem.at[0, 0]).wait_send()
        when(has["udy"[i]], sent)
    for i, d in enumerate(kinds):
        for owner in range(depth):
            for same in range(2):
                counts = [
                    sum(d in r[4] and r[1:3] == (owner, same) for r in events[k]) for k in range(depth)
                ]
                which = owner * 2 + (1 - same) + (2 * same - 1) * y
                for count in sorted(set(counts) - {0}):
                    def sent(count=count, i=i, d=d, which=which):
                        copy(d, 0, count * PIECE, send_sem.at[i, which], recv_sem.at[0, 0]).wait_send()
                    when([c == count for c in counts], sent)
    for which in range(2 * depth):
        copy("p", 0, rows, core_send.at[which], core_recv.at[which]).wait_send()


def solution(mesh):
    groups, n = mesh.shape["groups"], mesh.shape["dp"]
    depth = n // 4
    swap = groups % 2 == 0

    def local(tokens, base_weight, down_stack, up_stack, adapter_scale, lengths, adapter_ids):
        rows, base_cols = base_weight.shape
        cols = base_cols + down_stack.shape[1]
        pieces = rows // PIECE
        special = (5 * pieces) // 16 if swap else 0
        gathered = pieces - special
        first = tuple(range(gathered - pieces // 8, gathered))
        slots = 2 * depth
        any_space = pl.BlockSpec(memory_space=pl.ANY)
        scalars = pl.BlockSpec(memory_space=pltpu.SMEM)
        return pl.pallas_call(
            functools.partial(kernel, (depth, special, first, swap)),
            out_shape=jax.ShapeDtypeStruct((tokens.shape[0], base_cols), jnp.bfloat16),
            in_specs=[any_space] * 4 + [scalars] * 3,
            out_specs=pl.BlockSpec(memory_space=pltpu.VMEM),
            scratch_shapes=[
                pltpu.VMEM((n * rows, cols), jnp.bfloat16),
                pltpu.VMEM(tokens.shape, jnp.bfloat16),
                pltpu.VMEM(up_stack.shape, jnp.bfloat16),
                pltpu.VMEM((tokens.shape[0], cols), jnp.float32),
                pltpu.SemaphoreType.DMA((4,)),
                pltpu.SemaphoreType.DMA((slots, pieces)),
                pltpu.SemaphoreType.DMA((4, slots)),
                pltpu.SemaphoreType.DMA((3,)),
                pltpu.SemaphoreType.DMA((slots,)),
                pltpu.SemaphoreType.DMA((slots,)),
            ],
            compiler_params=pltpu.CompilerParams(
                collective_id=0, has_side_effects=True, vmem_limit_bytes=56 * 1024 * 1024
            ),
        )(tokens, base_weight, down_stack, up_stack, adapter_scale, lengths, adapter_ids)

    in_specs = (
        P(("groups", "dp"), None), P("dp", None), P("dp", None), P(), P(),
        P(("groups", "dp")), P(("groups", "dp")),
    )
    return jax.shard_map(
        local, mesh=mesh, in_specs=in_specs, out_specs=P(("groups", "dp"), None), check_vma=False
    )
```

```python
import functools

import jax
import jax.numpy as jnp
from jax import lax
from jax.experimental import pallas as pl
from jax.experimental.pallas import tpu as pltpu
from jax.sharding import PartitionSpec as P

BLOCK = 128
PIECE = 32
MESH = pl.DeviceIdType.MESH


def plan(depth, pieces, special, first):
    gathered = pieces - special
    queues = {
        (z, d): []
        for z in range(depth)
        for d in "udyx"
        if not (d == "u" and z == depth - 1) and not (d == "d" and z == 0)
    }

    def targets(piece, via):
        if via == "x":
            return ""
        if piece in first:
            out = {"own": "udy", "y": "ud", "u": "u", "d": "d"}[via]
        else:
            out = {"own": "udy", "y": "", "u": "uy", "d": "dy"}[via]
        return out + "x" if piece < special and via != "own" else out

    own = [targets(k, "own") for k in range(gathered)]
    for z in range(depth):
        for k in range(gathered):
            for d in own[k]:
                if (z, d) in queues:
                    queues[z, d].append((z, 1, k))
    events = [[] for _ in range(depth)]
    while any(queues.values()):
        moved = [(z, d, q.pop(0)) for (z, d), q in queues.items() if q]
        for z, d, (owner, same, k) in sorted(moved, key=lambda m: "udyx".index(m[1])):
            at = z + (d == "u") - (d == "d")
            if d == "y":
                same = 1 - same
            out = "".join(o for o in targets(k, d) if (at, o) in queues)
            for o in out:
                queues[at, o].append((owner, same, k))
            events[at].append((d, owner, same, k, out))
    return events


def kernel(
    sizes, tok_hbm, base_hbm, down_hbm, up_hbm, scale_ref, len_ref, ids_ref, out_ref,
    held, tok, up, acc, load_sem, recv_sem, send_sem, own_sem, core_recv, core_send,
):
    depth, special, first, swap = sizes
    rows, base_cols = base_hbm.shape
    pieces = rows // PIECE
    gathered = pieces - special
    events = plan(depth, pieces, special, first)
    group, me = lax.axis_index("groups"), lax.axis_index("dp")
    core, y, z = me % 2, (me // 2) % 2, me // 4
    side = group % 2
    at = [z == k for k in range(depth)]

    def pick(values):
        if len(set(values)) == 1:
            return values[0]
        out = jnp.int32(values[0])
        for k in range(1, depth):
            if values[k] != values[0]:
                out = jnp.where(at[k], jnp.int32(values[k]), out)
        return out

    def when(flags, fn):
        if all(flags):
            fn()
        elif any(flags):
            pl.when(pick([int(f) for f in flags]) == 1)(fn)

    peers = {
        "u": (group, me + 4),
        "d": (group, me - 4),
        "y": (group, me + 2 - 4 * y),
        "x": (group + 1 - 2 * side, me),
        "p": (group, me + 1 - 2 * core),
    }
    has = {
        "u": [k < depth - 1 for k in range(depth)],
        "d": [k > 0 for k in range(depth)],
        "y": [True] * depth,
        "x": [swap] * depth,
        "p": [True] * depth,
    }
    kinds = "udyx"

    pair = z * 2 + y
    mine = pl.multiple_of(me * rows, rows)
    loads = [
        pltpu.make_async_copy(base_hbm, held.at[pl.ds(mine, rows), pl.ds(0, base_cols)], load_sem.at[0]),
        pltpu.make_async_copy(
            down_hbm, held.at[pl.ds(mine, rows), pl.ds(base_cols, down_hbm.shape[1])], load_sem.at[1]
        ),
        pltpu.make_async_copy(tok_hbm, tok, load_sem.at[2]),
        pltpu.make_async_copy(up_hbm, up, load_sem.at[3]),
    ]
    for load in loads:
        load.start()

    barrier = pltpu.get_barrier_semaphore()
    for d in "udyxp":
        def greet(d=d):
            pl.semaphore_signal(barrier, inc=1, device_id=peers[d], device_id_type=MESH)
        when(has[d], greet)
    pl.semaphore_wait(barrier, pick([sum(has[d][k] for d in "udyxp") for k in range(depth)]))

    def copy(d, start, count, send, recv):
        piece = held.at[pl.ds(start, count)]
        return pltpu.make_async_remote_copy(
            src_ref=piece, dst_ref=piece, send_sem=send, recv_sem=recv,
            device_id=peers[d], device_id_type=MESH,
        )

    loads[0].wait()
    loads[1].wait()
    for k in range(gathered):
        sub = k + side * special if k < special else special + k
        start = pl.multiple_of(mine + sub * PIECE, PIECE)
        for i, d in enumerate("udy"):
            def send(i=i, d=d, start=start, sub=sub):
                copy(d, start, PIECE, own_sem.at[i], recv_sem.at[pair, sub]).start()
            when(has[d], send)
    blocks = core_recv.shape[1]
    deep = rows // blocks
    per_block = pieces // blocks
    for b in range(blocks):
        copy("p", pl.multiple_of(mine + b * deep, deep), deep, core_send.at[pair], core_recv.at[pair, b]).start()

    cols = held.shape[1]
    step = cols // 5 if cols % 5 == 0 else cols

    def multiply(which, block, fresh):
        copy("p", 0, deep, core_send.at[which], core_recv.at[which, block]).wait_recv()
        spans = [
            pl.ds(pl.multiple_of((which * 2 + c) * rows + block * deep, deep), deep) for c in range(2)
        ]
        left = jnp.concatenate([tok[:, span] for span in spans], axis=1)

        @pl.loop(0, cols // step)
        def _(n):
            part = pl.ds(pl.multiple_of(n * step, step), step)
            right = jnp.concatenate([held[span, part] for span in spans], axis=0)
            term = jnp.dot(left, right, preferred_element_type=jnp.float32)
            acc[:, part] = term if fresh else acc[:, part] + term

    def landed(side_of):
        order = []
        for row in events:
            seen, found = {}, []
            for e, (via, owner, same, k, _) in enumerate(row):
                if via == "x":
                    sub = (1 - side_of) * special + k
                else:
                    sub = side_of * special + k if k < special else special + k
                key = (owner, same, sub // per_block)
                seen[key] = seen.get(key, 0) + 1
                if seen[key] == per_block:
                    found.append((e, key))
            order.append(found)
        return order

    both = [landed(0), landed(1)]
    ready = []
    for k in range(depth):
        last = {}
        for found in (both[0][k], both[1][k]):
            for e, key in found:
                last[key] = max(last.get(key, 0), e)
        ready.append(sorted((e, key) for key, e in last.items()))
    due = {}
    for m in range(len(ready[0])):
        due.setdefault(max(r[m][0] for r in ready), []).append([r[m][1] for r in ready])
    total = len(events[0])
    for e in range(total):
        row = [events[k][e] for k in range(depth)]
        owner = pick([r[1] for r in row])
        same = pick([r[2] for r in row])
        offset, slope = [], []
        for r in row:
            if r[0] == "x":
                offset.append(special + r[3])
                slope.append(-special)
            elif r[3] < special:
                offset.append(r[3])
                slope.append(special)
            else:
                offset.append(special + r[3])
                slope.append(0)
        sub = pick(offset) + pick(slope) * side
        which = owner * 2 + (1 - same) + (2 * same - 1) * y
        start = pl.multiple_of((which * 2 + core) * rows + sub * PIECE, PIECE)
        arrived = recv_sem.at[which, sub]
        copy("p", start, PIECE, core_send.at[which], arrived).wait_recv()
        for i, d in enumerate(kinds):
            def relay(i=i, d=d, start=start, which=which, arrived=arrived):
                copy(d, start, PIECE, send_sem.at[i, which], arrived).start()
            when([d in r[4] for r in row], relay)
        block = sub // per_block if blocks > 1 else 0
        copy("p", start, PIECE, core_send.at[which], core_recv.at[which, block]).start()
        if e == 4:
            loads[2].wait()
            for b in range(blocks):
                multiply(pair, b, b == 0)
        for keys in due.get(e, []):
            owners, sames = pick([key[0] for key in keys]), pick([key[1] for key in keys])
            multiply(owners * 2 + (1 - sames) + (2 * sames - 1) * y, pick([key[2] for key in keys]), False)

    loads[3].wait()
    tokens = acc.shape[0]
    adapters = scale_ref.shape[0]
    rank = (cols - base_cols) // adapters
    boundary = ((len_ref[0] + (BLOCK - 1)) // BLOCK) * BLOCK
    position = lax.broadcasted_iota(jnp.int32, (tokens, 1), 0)
    second = position >= boundary
    offsets = jnp.where(second, position - boundary, position)
    live = offsets < jnp.where(second, len_ref[1], len_ref[0])
    low = jnp.where(second, ids_ref[1], ids_ref[0]) * rank
    scale = jnp.where(second, scale_ref[ids_ref[1]], scale_ref[ids_ref[0]])
    lane = lax.broadcasted_iota(jnp.int32, (tokens, cols - base_cols), 1)
    chosen = (lane >= low) & (lane < low + rank)
    widened = jnp.where(chosen, acc[:, base_cols:], 0.0).astype(jnp.bfloat16)
    width = base_cols // 3
    for n in range(3):
        part = slice(n * width, (n + 1) * width)
        adapter_out = jnp.dot(widened, up[:, part], preferred_element_type=jnp.float32)
        out_ref[:, part] = jnp.where(live, acc[:, part] + scale * adapter_out, 0.0).astype(out_ref.dtype)

    for i in range(3):
        def sent(i=i):
            copy("udy"[i], 0, gathered * PIECE, own_sem.at[i], recv_sem.at[0, 0]).wait_send()
        when(has["udy"[i]], sent)
    for i, d in enumerate(kinds):
        for owner in range(depth):
            for same in range(2):
                counts = [
                    sum(d in r[4] and r[1:3] == (owner, same) for r in events[k]) for k in range(depth)
                ]
                which = owner * 2 + (1 - same) + (2 * same - 1) * y
                for count in sorted(set(counts) - {0}):
                    def sent(count=count, i=i, d=d, which=which):
                        copy(d, 0, count * PIECE, send_sem.at[i, which], recv_sem.at[0, 0]).wait_send()
                    when([c == count for c in counts], sent)
    for which in range(2 * depth):
        copy("p", 0, rows, core_send.at[which], core_recv.at[which, 0]).wait_send()


def solution(mesh):
    groups, n = mesh.shape["groups"], mesh.shape["dp"]
    depth = n // 4
    swap = groups % 2 == 0

    def local(tokens, base_weight, down_stack, up_stack, adapter_scale, lengths, adapter_ids):
        rows, base_cols = base_weight.shape
        cols = base_cols + down_stack.shape[1]
        pieces = rows // PIECE
        special = (5 * pieces) // 16 if swap else 0
        gathered = pieces - special
        first = tuple(range(gathered - pieces // 8, gathered))
        slots = 2 * depth
        any_space = pl.BlockSpec(memory_space=pl.ANY)
        scalars = pl.BlockSpec(memory_space=pltpu.SMEM)
        return pl.pallas_call(
            functools.partial(kernel, (depth, special, first, swap)),
            out_shape=jax.ShapeDtypeStruct((tokens.shape[0], base_cols), jnp.bfloat16),
            in_specs=[any_space] * 4 + [scalars] * 3,
            out_specs=pl.BlockSpec(memory_space=pltpu.VMEM),
            scratch_shapes=[
                pltpu.VMEM((n * rows, cols), jnp.bfloat16),
                pltpu.VMEM(tokens.shape, jnp.bfloat16),
                pltpu.VMEM(up_stack.shape, jnp.bfloat16),
                pltpu.VMEM((tokens.shape[0], cols), jnp.float32),
                pltpu.SemaphoreType.DMA((4,)),
                pltpu.SemaphoreType.DMA((slots, pieces)),
                pltpu.SemaphoreType.DMA((4, slots)),
                pltpu.SemaphoreType.DMA((3,)),
                pltpu.SemaphoreType.DMA((slots, max(1, rows // 256))),
                pltpu.SemaphoreType.DMA((slots,)),
            ],
            compiler_params=pltpu.CompilerParams(
                collective_id=0, has_side_effects=True, vmem_limit_bytes=56 * 1024 * 1024
            ),
        )(tokens, base_weight, down_stack, up_stack, adapter_scale, lengths, adapter_ids)

    in_specs = (
        P(("groups", "dp"), None), P("dp", None), P("dp", None), P(), P(),
        P(("groups", "dp")), P(("groups", "dp")),
    )
    return jax.shard_map(
        local, mesh=mesh, in_specs=in_specs, out_specs=P(("groups", "dp"), None), check_vma=False
    )
```

```python
import functools

import jax
import jax.numpy as jnp
from jax import lax
from jax.experimental import pallas as pl
from jax.experimental.pallas import tpu as pltpu
from jax.sharding import PartitionSpec as P

BLOCK = 128
PIECE = 32
MESH = pl.DeviceIdType.MESH


def plan(depth, pieces, special, first):
    gathered = pieces - special
    queues = {
        (z, d): []
        for z in range(depth)
        for d in "udyx"
        if not (d == "u" and z == depth - 1) and not (d == "d" and z == 0)
    }

    def targets(piece, via):
        if via == "x":
            return ""
        if piece in first:
            out = {"own": "udy", "y": "ud", "u": "u", "d": "d"}[via]
        else:
            out = {"own": "udy", "y": "", "u": "uy", "d": "dy"}[via]
        return out + "x" if piece < special and via != "own" else out

    own = [targets(k, "own") for k in range(gathered)]
    for z in range(depth):
        for k in range(gathered):
            for d in own[k]:
                if (z, d) in queues:
                    queues[z, d].append((z, 1, k))
    events = [[] for _ in range(depth)]
    while any(queues.values()):
        moved = [(z, d, q.pop(0)) for (z, d), q in queues.items() if q]
        for z, d, (owner, same, k) in sorted(moved, key=lambda m: "udyx".index(m[1])):
            at = z + (d == "u") - (d == "d")
            if d == "y":
                same = 1 - same
            out = "".join(o for o in targets(k, d) if (at, o) in queues)
            for o in out:
                queues[at, o].append((owner, same, k))
            events[at].append((d, owner, same, k, out))
    return events


def kernel(
    sizes, tok_hbm, base_hbm, down_hbm, up_hbm, scale_ref, len_ref, ids_ref, out_ref,
    held, tok, up, acc, load_sem, recv_sem, send_sem, own_sem, core_recv, core_send,
):
    depth, special, first, swap = sizes
    rows, base_cols = base_hbm.shape
    pieces = rows // PIECE
    gathered = pieces - special
    events = plan(depth, pieces, special, first)
    group, me = lax.axis_index("groups"), lax.axis_index("dp")
    core, y, z = me % 2, (me // 2) % 2, me // 4
    side = group % 2
    at = [z == k for k in range(depth)]

    def pick(values):
        if len(set(values)) == 1:
            return values[0]
        out = jnp.int32(values[0])
        for k in range(1, depth):
            if values[k] != values[0]:
                out = jnp.where(at[k], jnp.int32(values[k]), out)
        return out

    def when(flags, fn):
        if all(flags):
            fn()
        elif any(flags):
            pl.when(pick([int(f) for f in flags]) == 1)(fn)

    peers = {
        "u": (group, me + 4),
        "d": (group, me - 4),
        "y": (group, me + 2 - 4 * y),
        "x": (group + 1 - 2 * side, me),
        "p": (group, me + 1 - 2 * core),
    }
    has = {
        "u": [k < depth - 1 for k in range(depth)],
        "d": [k > 0 for k in range(depth)],
        "y": [True] * depth,
        "x": [swap] * depth,
        "p": [True] * depth,
    }
    kinds = "udyx"

    pair = z * 2 + y
    mine = pl.multiple_of(me * rows, rows)
    loads = [
        pltpu.make_async_copy(base_hbm, held.at[pl.ds(mine, rows), pl.ds(0, base_cols)], load_sem.at[0]),
        pltpu.make_async_copy(
            down_hbm, held.at[pl.ds(mine, rows), pl.ds(base_cols, down_hbm.shape[1])], load_sem.at[1]
        ),
        pltpu.make_async_copy(tok_hbm, tok, load_sem.at[2]),
        pltpu.make_async_copy(up_hbm, up, load_sem.at[3]),
    ]
    for load in loads:
        load.start()

    barrier = pltpu.get_barrier_semaphore()
    for d in "udyxp":
        def greet(d=d):
            pl.semaphore_signal(barrier, inc=1, device_id=peers[d], device_id_type=MESH)
        when(has[d], greet)
    pl.semaphore_wait(barrier, pick([sum(has[d][k] for d in "udyxp") for k in range(depth)]))

    def copy(d, start, count, send, recv):
        piece = held.at[pl.ds(start, count)]
        return pltpu.make_async_remote_copy(
            src_ref=piece, dst_ref=piece, send_sem=send, recv_sem=recv,
            device_id=peers[d], device_id_type=MESH,
        )

    loads[0].wait()
    loads[1].wait()
    for k in range(gathered):
        sub = k + side * special if k < special else special + k
        start = pl.multiple_of(mine + sub * PIECE, PIECE)
        for i, d in enumerate("udy"):
            def send(i=i, d=d, start=start, sub=sub):
                copy(d, start, PIECE, own_sem.at[i], recv_sem.at[pair, sub]).start()
            when(has[d], send)
    blocks = core_recv.shape[1]
    deep = rows // blocks
    per_block = pieces // blocks
    for b in range(blocks):
        copy("p", pl.multiple_of(mine + b * deep, deep), deep, core_send.at[pair], core_recv.at[pair, b]).start()

    cols = held.shape[1]

    def multiply(which, block, fresh):
        copy("p", 0, deep, core_send.at[which], core_recv.at[which, block]).wait_recv()
        spans = [
            pl.ds(pl.multiple_of((which * 2 + c) * rows + block * deep, deep), deep) for c in range(2)
        ]

        term = sum(jnp.dot(tok[:, span], held[span, :], preferred_element_type=jnp.float32) for span in spans)
        acc[...] = term if fresh else acc[...] + term

    def landed(side_of):
        order = []
        for row in events:
            seen, found = {}, []
            for e, (via, owner, same, k, _) in enumerate(row):
                if via == "x":
                    sub = (1 - side_of) * special + k
                else:
                    sub = side_of * special + k if k < special else special + k
                key = (owner, same, sub // per_block)
                seen[key] = seen.get(key, 0) + 1
                if seen[key] == per_block:
                    found.append((e, key))
            order.append(found)
        return order

    both = [landed(0), landed(1)]
    ready = []
    for k in range(depth):
        last = {}
        for found in (both[0][k], both[1][k]):
            for e, key in found:
                last[key] = max(last.get(key, 0), e)
        ready.append(sorted((e, key) for key, e in last.items()))
    due = {}
    for m in range(len(ready[0])):
        due.setdefault(max(r[m][0] for r in ready), []).append([r[m][1] for r in ready])
    total = len(events[0])
    for e in range(total):
        row = [events[k][e] for k in range(depth)]
        owner = pick([r[1] for r in row])
        same = pick([r[2] for r in row])
        offset, slope = [], []
        for r in row:
            if r[0] == "x":
                offset.append(special + r[3])
                slope.append(-special)
            elif r[3] < special:
                offset.append(r[3])
                slope.append(special)
            else:
                offset.append(special + r[3])
                slope.append(0)
        sub = pick(offset) + pick(slope) * side
        which = owner * 2 + (1 - same) + (2 * same - 1) * y
        start = pl.multiple_of((which * 2 + core) * rows + sub * PIECE, PIECE)
        arrived = recv_sem.at[which, sub]
        copy("p", start, PIECE, core_send.at[which], arrived).wait_recv()
        for i, d in enumerate(kinds):
            def relay(i=i, d=d, start=start, which=which, arrived=arrived):
                copy(d, start, PIECE, send_sem.at[i, which], arrived).start()
            when([d in r[4] for r in row], relay)
        block = sub // per_block if blocks > 1 else 0
        copy("p", start, PIECE, core_send.at[which], core_recv.at[which, block]).start()
        if e == 4:
            loads[2].wait()
            for b in range(blocks):
                multiply(pair, b, b == 0)
        for keys in due.get(e, []):
            owners, sames = pick([key[0] for key in keys]), pick([key[1] for key in keys])
            multiply(owners * 2 + (1 - sames) + (2 * sames - 1) * y, pick([key[2] for key in keys]), False)

    loads[3].wait()
    tokens = acc.shape[0]
    adapters = scale_ref.shape[0]
    rank = (cols - base_cols) // adapters
    boundary = ((len_ref[0] + (BLOCK - 1)) // BLOCK) * BLOCK
    position = lax.broadcasted_iota(jnp.int32, (tokens, 1), 0)
    second = position >= boundary
    offsets = jnp.where(second, position - boundary, position)
    live = offsets < jnp.where(second, len_ref[1], len_ref[0])
    low = jnp.where(second, ids_ref[1], ids_ref[0]) * rank
    scale = jnp.where(second, scale_ref[ids_ref[1]], scale_ref[ids_ref[0]])
    lane = lax.broadcasted_iota(jnp.int32, (tokens, cols - base_cols), 1)
    chosen = (lane >= low) & (lane < low + rank)
    widened = jnp.where(chosen, acc[:, base_cols:], 0.0).astype(jnp.bfloat16)
    width = base_cols // 3
    for n in range(3):
        part = slice(n * width, (n + 1) * width)
        adapter_out = jnp.dot(widened, up[:, part], preferred_element_type=jnp.float32)
        out_ref[:, part] = jnp.where(live, acc[:, part] + scale * adapter_out, 0.0).astype(out_ref.dtype)

    for i in range(3):
        def sent(i=i):
            copy("udy"[i], 0, gathered * PIECE, own_sem.at[i], recv_sem.at[0, 0]).wait_send()
        when(has["udy"[i]], sent)
    for i, d in enumerate(kinds):
        for owner in range(depth):
            for same in range(2):
                counts = [
                    sum(d in r[4] and r[1:3] == (owner, same) for r in events[k]) for k in range(depth)
                ]
                which = owner * 2 + (1 - same) + (2 * same - 1) * y
                for count in sorted(set(counts) - {0}):
                    def sent(count=count, i=i, d=d, which=which):
                        copy(d, 0, count * PIECE, send_sem.at[i, which], recv_sem.at[0, 0]).wait_send()
                    when([c == count for c in counts], sent)
    for which in range(2 * depth):
        copy("p", 0, rows, core_send.at[which], core_recv.at[which, 0]).wait_send()


def solution(mesh):
    groups, n = mesh.shape["groups"], mesh.shape["dp"]
    depth = n // 4
    swap = groups % 2 == 0

    def local(tokens, base_weight, down_stack, up_stack, adapter_scale, lengths, adapter_ids):
        rows, base_cols = base_weight.shape
        cols = base_cols + down_stack.shape[1]
        pieces = rows // PIECE
        special = (5 * pieces) // 16 if swap else 0
        gathered = pieces - special
        first = tuple(range(gathered - pieces // 8, gathered))
        slots = 2 * depth
        any_space = pl.BlockSpec(memory_space=pl.ANY)
        scalars = pl.BlockSpec(memory_space=pltpu.SMEM)
        return pl.pallas_call(
            functools.partial(kernel, (depth, special, first, swap)),
            out_shape=jax.ShapeDtypeStruct((tokens.shape[0], base_cols), jnp.bfloat16),
            in_specs=[any_space] * 4 + [scalars] * 3,
            out_specs=pl.BlockSpec(memory_space=pltpu.VMEM),
            scratch_shapes=[
                pltpu.VMEM((n * rows, cols), jnp.bfloat16),
                pltpu.VMEM(tokens.shape, jnp.bfloat16),
                pltpu.VMEM(up_stack.shape, jnp.bfloat16),
                pltpu.VMEM((tokens.shape[0], cols), jnp.float32),
                pltpu.SemaphoreType.DMA((4,)),
                pltpu.SemaphoreType.DMA((slots, pieces)),
                pltpu.SemaphoreType.DMA((4, slots)),
                pltpu.SemaphoreType.DMA((3,)),
                pltpu.SemaphoreType.DMA((slots, max(1, rows // 256))),
                pltpu.SemaphoreType.DMA((slots,)),
            ],
            compiler_params=pltpu.CompilerParams(
                collective_id=0, has_side_effects=True, vmem_limit_bytes=56 * 1024 * 1024
            ),
        )(tokens, base_weight, down_stack, up_stack, adapter_scale, lengths, adapter_ids)

    in_specs = (
        P(("groups", "dp"), None), P("dp", None), P("dp", None), P(), P(),
        P(("groups", "dp")), P(("groups", "dp")),
    )
    return jax.shard_map(
        local, mesh=mesh, in_specs=in_specs, out_specs=P(("groups", "dp"), None), check_vma=False
    )
```
